32 devices in a mesh: win: 2 (over y), tm: 4 (over z), row: 2 (over x), col: 2 (over core).
Axes of the slice: x: 2, y: 2, z: 4, core: 2. Of those that a mesh axis runs over, the one named last changes fastest.
Arguments:
- seams: bfloat16 [8, 3, 576, 1920], P(('win', 'tm'), None, 'row', 'col'), parts along dimension 0, may hold values from -24 to 24
- levels: int32 [8, 8, 16], P(('win', 'tm'), 'row', 'col'), parts along dimension 0, may hold values from 0 to 4
- weights: int32 [8], P('win'), parts along dimension 0, may hold values from 16 to 2047
Outputs:
- correction: float32 [8, 3, 576, 1920], P(('win', 'tm'), None, 'row', 'col'), parts along dimension 0
The draws below stay inside these ranges and needn't reach their ends.
There are 2 independent parts, one for each index of `win`. The reference program is written for one: setup_inputs(seed, part) draws one part's arguments, and reference() takes and returns one part's arrays. A program takes and returns all parts, laid end to end along the dimension named above; each array names one. Nothing has to cross between parts.
All inputs are finite; a program needn't handle non-finite values.
Results may differ from the reference program's by a relative error of at most 0.0064.
Values may be sent and summed in bfloat16 or wider, within the bound.
A program may use at most 64 MiB of HBM per device.

```python
import math
import jax
import jax.numpy as jnp
from jax import lax

C = 3
H = 576
W = 1920
GH = 8
GW = 16
FRAMES = 4


def draw_seams(key, part):
    key_base = jax.random.fold_in(key, 11)
    key_noise = jax.random.fold_in(key, 12)
    key_colp = jax.random.fold_in(key, 13)
    key_rowp = jax.random.fold_in(key, 14)
    key_phase = jax.random.fold_in(key, 15)
    col_period = 4 + jax.random.randint(key_colp, (C,), 0, 3)
    row_period = 4 + 2 * jax.random.randint(key_rowp, (C,), 0, 2)
    phases = jax.random.uniform(key_phase, (2, C), jnp.float32, 0.0, 2.0 * math.pi)
    col_ids = jnp.arange(W, dtype=jnp.int32)
    row_ids = jnp.arange(H, dtype=jnp.int32)
    col_frac = (col_ids[None, :] % col_period[:, None]).astype(jnp.float32) / col_period[:, None].astype(jnp.float32)
    row_frac = (row_ids[None, :] % row_period[:, None]).astype(jnp.float32) / row_period[:, None].astype(jnp.float32)
    col_wave = jnp.cos(2.0 * math.pi * col_frac + phases[0][:, None])
    row_wave = jnp.cos(2.0 * math.pi * row_frac + phases[1][:, None])
    base = jax.random.normal(key_base, (C, H, W), jnp.float32) * 0.35
    noise = jax.random.normal(key_noise, (FRAMES, C, H, W), jnp.float32) * 3.0
    stripes = 4.0 * col_wave[:, None, :] + 4.0 * row_wave[:, :, None]
    return jnp.clip(base[None] + stripes[None] + noise, -24.0, 24.0).astype(jnp.bfloat16)


def set_ends(result, key, low, high):
    index_at = [jax.random.randint(jax.random.fold_in(key, axis), (), 0, length) for axis, length in enumerate(result.shape)]
    widest = result.shape.index(max(result.shape))
    beside = index_at[:widest] + [(index_at[widest] + 1) % result.shape[widest]] + index_at[widest + 1:]
    return result.at[tuple(index_at)].set(low).at[tuple(beside)].set(high)


def setup_inputs(seed: int = 0, part: int = 0) -> dict:
    streams_of = jax.random.split(jax.random.key(seed), 4)
    own_keys = jax.random.split(jax.random.fold_in(streams_of[3], part), 4)
    seams = draw_seams(jax.random.fold_in(jax.random.fold_in(streams_of[3], part), 71), part)
    levels = set_ends(jax.random.randint(own_keys[1], (FRAMES, GH, GW), 0, 5), jax.random.fold_in(own_keys[1], 1), 0, 4).astype(jnp.int32)
    weights = set_ends(jax.random.randint(own_keys[2], (FRAMES,), 16, 2048), jax.random.fold_in(own_keys[2], 1), 16, 2047).astype(jnp.int32)
    return dict(seams=seams, levels=levels, weights=weights)


screen = 0.001

def cosine_table(length_all, mode_first, mode_count, cell_first, cell_count):
    mode_ids = mode_first + jnp.arange(mode_count, dtype=jnp.int32)
    cell_ids = cell_first + jnp.arange(cell_count, dtype=jnp.int32)
    phases = (2 * cell_ids[None, :] + 1) * mode_ids[:, None] % (4 * length_all)
    angles = phases.astype(jnp.float32) * (math.pi / (2.0 * length_all))
    scales = jnp.where(mode_ids == 0, math.sqrt(1.0 / length_all), math.sqrt(2.0 / length_all)).astype(jnp.float32)
    return (jnp.cos(angles) * scales[:, None]).astype(jnp.bfloat16)

def laplace_eigen(length_all, mode_first, mode_count):
    mode_ids = (mode_first + jnp.arange(mode_count, dtype=jnp.int32)).astype(jnp.float32)
    sines = jnp.sin(mode_ids * (math.pi / (2.0 * length_all)))
    return 4.0 * sines * sines

def couplings(weights):
    stiff = weights.astype(jnp.float32) / 256.0
    couple = 2.0 * stiff[:-1] * stiff[1:] / (stiff[:-1] + stiff[1:])
    zeroes = jnp.zeros((1,), jnp.float32)
    return (jnp.concatenate([zeroes, couple]), jnp.concatenate([couple, zeroes]))

def reference(seams, levels, weights):
    frames, channels, full_height, full_width = seams.shape
    tile_rows = full_height // levels.shape[1]
    tile_cols = full_width // levels.shape[2]
    tile_level = jnp.repeat(jnp.repeat(levels.astype(jnp.float32) * 0.25, tile_rows, axis=1), tile_cols, axis=2)
    blended = (seams.astype(jnp.float32) * tile_level[:, None]).astype(jnp.bfloat16)
    table_w = cosine_table(full_width, 0, full_width, 0, full_width).astype(jnp.float32)
    table_h = cosine_table(full_height, 0, full_height, 0, full_height).astype(jnp.float32)
    highest = lax.Precision.HIGHEST
    spectrum_w = jnp.einsum('fchw,kw->fchk', blended.astype(jnp.float32), table_w, precision=highest).astype(jnp.bfloat16)
    spectrum = jnp.einsum('qh,fchk->fcqk', table_h, spectrum_w.astype(jnp.float32), precision=highest)
    eigen_sum = laplace_eigen(full_height, 0, full_height)[:, None] + laplace_eigen(full_width, 0, full_width)[None, :]
    couple_below, couple_above = couplings(weights)
    ratio_prev = jnp.zeros((full_height, full_width), jnp.float32)
    value_prev = jnp.zeros((channels, full_height, full_width), jnp.float32)
    reduced_all = []
    ratio_all = []
    for frame in range(frames):
        pivot = screen + eigen_sum + couple_below[frame] + couple_above[frame] - couple_below[frame] * ratio_prev
        value_now = (spectrum[frame] + couple_below[frame] * value_prev) / pivot
        ratio_prev = couple_above[frame] / pivot
        reduced_all.append(value_now)
        ratio_all.append(ratio_prev)
        value_prev = value_now
    solved_all = [None] * frames
    following = jnp.zeros((channels, full_height, full_width), jnp.float32)
    for frame in range(frames - 1, -1, -1):
        following = reduced_all[frame] + ratio_all[frame] * following
        solved_all[frame] = following
    solved = jnp.stack(solved_all).astype(jnp.bfloat16)
    restored = jnp.einsum('qh,fcqk->fchk', table_h, solved.astype(jnp.float32), precision=highest).astype(jnp.bfloat16)
    return jnp.einsum('fchk,kw->fchw', restored.astype(jnp.float32), table_w, precision=highest)
```

```python
import functools
import math

import jax
import jax.numpy as jnp
from jax import lax
from jax.experimental import pallas as pl
from jax.experimental.pallas import tpu as pltpu
from jax.sharding import PartitionSpec as P

screen = 0.001
LANES = 128
MESH = pl.DeviceIdType.MESH


def scales_of(length_all, mode_ids, valid=None):
    scales = jnp.where(
        mode_ids == 0, math.sqrt(1.0 / length_all), math.sqrt(2.0 / length_all)
    ).astype(jnp.float32)
    return scales if valid is None else jnp.where(valid, scales, 0.0)


def angles_of(length_all, products):
    return (products % (4 * length_all)).astype(jnp.float32) * (math.pi / (2.0 * length_all))


def table_cells_by_modes(length_all, cell_first, cell_count, mode_ids, scales):
    step = 24
    mode_ids = mode_ids[..., None, :]
    coarse = 2 * step * jnp.arange(cell_count // step, dtype=jnp.int32)[:, None]
    fine = 2 * (cell_first + jnp.arange(step, dtype=jnp.int32))[:, None] + 1
    angle_a = angles_of(length_all, coarse * mode_ids)
    angle_b = angles_of(length_all, fine * mode_ids)
    scales = scales[..., None, :]
    cos_a, sin_a = jnp.cos(angle_a), jnp.sin(angle_a)
    cos_b, sin_b = jnp.cos(angle_b) * scales, jnp.sin(angle_b) * scales
    table = (
        cos_a[..., :, None, :] * cos_b[..., None, :, :]
        - sin_a[..., :, None, :] * sin_b[..., None, :, :]
    )
    return table.reshape(table.shape[:-3] + (cell_count, table.shape[-1])).astype(jnp.bfloat16)


def table_modes_by_cells(length_all, bases, step, scales, cell_first, cell_count):
    odd = 2 * (cell_first + jnp.arange(cell_count, dtype=jnp.int32))[None, :] + 1
    angle_a = angles_of(length_all, bases[:, None] * odd)
    angle_b = angles_of(length_all, jnp.arange(step, dtype=jnp.int32)[:, None] * odd)
    cos_a, sin_a = jnp.cos(angle_a), jnp.sin(angle_a)
    cos_b, sin_b = jnp.cos(angle_b), jnp.sin(angle_b)
    table = cos_a[:, None] * cos_b[None] - sin_a[:, None] * sin_b[None]
    table = table * scales[:, :, None]
    return table.reshape(-1, cell_count).astype(jnp.bfloat16)


def laplace_eigen(length_all, mode_ids):
    sines = jnp.sin(mode_ids.astype(jnp.float32) * (math.pi / (2.0 * length_all)))
    return 4.0 * sines * sines


def kernel(J, R, n, C, M, x_ref, twf, twb, thf, tht, dd, ee, cpl, o_ref,
           xg, sw, sr, u, yb, yin, zin, xb, rb, rg, out,
           g_s, g_r, f_s, f_r, y_s, y_r, z_r, x_s, b_s, b_r, c_s, c_r, o_s):
    j, r, t = lax.axis_index("col"), lax.axis_index("row"), lax.axis_index("tm")
    N = C * M
    left = t < n // 2
    p = jnp.where(left, t, n - 1 - t)
    inner = jnp.where(left, t + 1, t - 1)
    outer = jnp.where(left, t - 1, t + 1)
    edge = p == 0
    mid = p == n // 2 - 1

    barrier = pltpu.get_barrier_semaphore()
    for d in range(1, J):
        pl.semaphore_signal(barrier, 1, device_id={"col": lax.rem(j + d, J)}, device_id_type=MESH)
    for d in range(1, R):
        pl.semaphore_signal(barrier, 1, device_id={"row": lax.rem(r + d, R)}, device_id_type=MESH)
    pl.semaphore_signal(barrier, 1, device_id={"tm": inner}, device_id_type=MESH)

    @pl.when(p > 0)
    def _():
        pl.semaphore_signal(barrier, 1, device_id={"tm": outer}, device_id_type=MESH)
        pl.semaphore_wait(barrier, J + R)

    @pl.when(p == 0)
    def _():
        pl.semaphore_wait(barrier, J + R - 1)

    def remote(src, dst, ss, rs, where):
        return pltpu.make_async_remote_copy(
            src_ref=src, dst_ref=dst, send_sem=ss, recv_sem=rs,
            device_id=where, device_id_type=MESH)

    def slot(jj, rr, m):
        return pl.ds(pl.multiple_of(((jj * R + rr) * M + m) * LANES, LANES), LANES)

    def gather(c, d):
        return remote(x_ref.at[c], xg.at[c, d - 1], g_s.at[c, d - 1], g_r.at[c, d - 1],
                      {"col": lax.rem(j + d, J)})

    def row_out(i, d):
        peer = lax.rem(r + d, R)
        return remote(sw.at[i, peer], sr.at[i, d - 1], f_s.at[i, d - 1], f_r.at[i, d - 1],
                      {"row": peer})

    def y_inner(i):
        return remote(yb.at[i], yin.at[i], y_s.at[i], y_r.at[i], {"tm": inner})

    def y_middle(i):
        return remote(yb.at[i], zin.at[i], y_s.at[i], z_r.at[i], {"tm": inner})

    def x_outer(i):
        return remote(xb.at[i], zin.at[i], x_s.at[i], z_r.at[i], {"tm": outer})

    def row_back(i, c, m, d):
        return remote(rb.at[i, d - 1], rg.at[c, :, slot(j, r, m)], b_s.at[i, d - 1],
                      b_r.at[i, d - 1], {"row": lax.rem(r + d, R)})

    def col_share(i, c, m, d, e):
        part = rg.at[c, :, slot(j, lax.rem(r + R - d, R), m)]
        return remote(part, part, c_s.at[i, d, e - 1], c_r.at[i, d, e - 1],
                      {"col": lax.rem(j + e, J)})

    def out_copy(c):
        return pltpu.make_async_copy(out.at[c], o_ref.at[c], o_s.at[c])

    for c in range(C):
        for d in range(1, J):
            gather(c, d).start()

    def dot(a, b):
        return jnp.dot(a, b, preferred_element_type=jnp.float32)

    def step(i, carry):
        @pl.when(i < N)
        def _():
            c, m = i // M, i % M

            @pl.when(m == 0)
            def _():
                for d in range(1, J):
                    gather(c, d).wait_recv()
            acc = dot(x_ref[c], twf[0, m])
            for d in range(1, J):
                acc += dot(xg[c, d - 1], twf[d, m])
            low = acc.astype(jnp.bfloat16)
            for rr in range(R):
                sw[i, rr] = low[:, rr * LANES:(rr + 1) * LANES]
            for d in range(1, R):
                row_out(i, d).start()

        ib = i - 1

        @pl.when((ib >= 0) & (ib < N))
        def _():
            acc = dot(thf[r], sw[ib, r])
            for d in range(1, R):
                row_out(ib, d).wait_recv()
                acc += dot(thf[lax.rem(r + R - d, R)], sr[ib, d - 1])
            u[ib] = acc

        ic = i - 1 - p

        @pl.when((ic >= 0) & (ic < N))
        def _():
            @pl.when(p > 0)
            def _():
                y_inner(ic).wait_recv()
                u[ic] = u[ic] + cpl[0] * yin[ic].astype(jnp.float32)
            yb[ic] = (u[ic] * dd[ic % M]).astype(jnp.bfloat16)

            @pl.when(mid)
            def _():
                y_middle(ic).start()

            @pl.when(jnp.logical_not(mid))
            def _():
                y_inner(ic).start()

        ix = i - n + p

        @pl.when((ix >= 0) & (ix < N))
        def _():
            c, m = ix // M, ix % M
            x_outer(ix).wait_recv()
            x = ((u[ix] + cpl[1] * zin[ix].astype(jnp.float32)) * ee[m]).astype(jnp.bfloat16)
            xb[ix] = x

            @pl.when(p > 0)
            def _():
                x_outer(ix).start()
            for d in range(1, R):
                rb[ix, d - 1] = dot(tht[lax.rem(r + d, R)], x).astype(jnp.bfloat16)
                row_back(ix, c, m, d).start()
            rg[c, :, slot(j, r, m)] = dot(tht[r], x).astype(jnp.bfloat16)
            for e in range(1, J):
                col_share(ix, c, m, 0, e).start()

        iw = ix - 1

        @pl.when((iw >= 0) & (iw < N))
        def _():
            c, m = iw // M, iw % M
            for d in range(1, R):
                row_back(iw, c, m, d).wait_recv()
                for e in range(1, J):
                    col_share(iw, c, m, d, e).start()

        ig = ix - 2

        @pl.when((ig >= 0) & (ig < N))
        def _():
            c, m = ig // M, ig % M
            for d in range(R):
                for e in range(1, J):
                    col_share(ig, c, m, d, e).wait_recv()

            @pl.when(m == M - 1)
            def _():
                out[c] = dot(rg[c], twb[...])
                out_copy(c).start()
        return carry

    lax.fori_loop(0, N + n + 2, step, 0)

    def drain(i, carry):
        c, m = i // M, i % M
        for d in range(1, R):
            row_out(i, d).wait_send()
            row_back(i, c, m, d).wait_send()
        for d in range(R):
            for e in range(1, J):
                col_share(i, c, m, d, e).wait_send()
        y_inner(i).wait_send()

        @pl.when(p > 0)
        def _():
            x_outer(i).wait_send()
        return carry

    lax.fori_loop(0, N, drain, 0)
    for c in range(C):
        for d in range(1, J):
            gather(c, d).wait_send()
        out_copy(c).wait()


def local(seams, levels, weights):
    _, C, rows, cols = seams.shape
    R, J, n = lax.axis_size("row"), lax.axis_size("col"), lax.axis_size("tm")
    j, r, t = lax.axis_index("col"), lax.axis_index("row"), lax.axis_index("tm")
    H, W = rows * R, cols * J
    tile_rows, tile_cols = rows // levels.shape[1], cols // levels.shape[2]
    grid = levels[0].astype(jnp.float32) * 0.25
    grid = jnp.broadcast_to(
        grid[:, None, :, None], (levels.shape[1], tile_rows, levels.shape[2], tile_cols)
    ).reshape(rows, cols)
    blended = (seams[0].astype(jnp.float32) * grid[None]).astype(jnp.bfloat16)

    modes = W // (J * R)
    M = -(-modes // LANES)
    N = C * M
    lanes = jnp.arange(M * LANES, dtype=jnp.int32).reshape(M, LANES)
    valid = lanes < modes
    blocks = jnp.arange(R, dtype=jnp.int32)[None, :, None] * modes
    mode_f = (j * R * modes + blocks + lanes[:, None, :]).reshape(M, R * LANES)
    valid_f = jnp.broadcast_to(valid[:, None, :], (M, R, LANES)).reshape(M, R * LANES)
    scale_f = scales_of(W, mode_f, valid_f)
    twf = jnp.stack([
        table_cells_by_modes(W, lax.rem(j + J - d, J) * cols, cols, mode_f, scale_f)
        for d in range(J)])

    fine = 16
    bases = (jnp.arange(J * R, dtype=jnp.int32)[:, None] * modes
             + jnp.arange(M * LANES // fine, dtype=jnp.int32)[None, :] * fine).reshape(-1)
    mode_b = (jnp.arange(J * R, dtype=jnp.int32)[:, None] * modes
              + jnp.arange(M * LANES, dtype=jnp.int32)[None, :])
    valid_b = jnp.broadcast_to(valid.reshape(1, -1), mode_b.shape)
    scale_b = scales_of(W, mode_b, valid_b).reshape(-1, fine)
    twb = table_modes_by_cells(W, bases, fine, scale_b, j * cols, cols)

    mode_h = jnp.arange(H, dtype=jnp.int32)
    tht = table_cells_by_modes(H, 0, H, mode_h, scales_of(H, mode_h))
    thf = tht.T.reshape(H, R, rows).transpose(1, 0, 2)
    tht = tht.reshape(R, rows, H)

    own_modes = (j * R + r) * modes + lanes
    a = (screen + laplace_eigen(H, mode_h)[None, :, None]
         + laplace_eigen(W, own_modes)[:, None, :])
    stiff = weights.astype(jnp.float32) / 256.0
    couple = 2.0 * stiff[:-1] * stiff[1:] / (stiff[:-1] + stiff[1:])
    half = n // 2
    left = t < half
    place = jnp.where(left, t, n - 1 - t)
    ends = jnp.concatenate([jnp.zeros((1,), jnp.float32), couple])
    flipped = jnp.concatenate([jnp.zeros((1,), jnp.float32), couple[::-1]])
    own = jnp.where(left, ends, flipped)
    other = jnp.where(left, flipped, ends)

    def sweep(chain):
        rest = jnp.zeros_like(a)
        first = None
        for k in range(half):
            base = a + chain[k] * rest
            inverse = 1.0 / (base + chain[k + 1])
            first = inverse if first is None else jnp.where(place == k, inverse, first)
            rest = base * inverse
        return base, rest, first

    base, _, dd = sweep(own)
    _, rest_other, _ = sweep(other)
    ee = jnp.where(place == half - 1, 1.0 / (base + own[half] * rest_other), dd)
    cpl = lax.dynamic_slice(own, (place,), (2,))

    bf, f32 = jnp.bfloat16, jnp.float32
    vm, dma = pltpu.VMEM, pltpu.SemaphoreType.DMA
    spec = pl.BlockSpec(memory_space=pltpu.VMEM)
    result = pl.pallas_call(
        functools.partial(kernel, J, R, n, C, M),
        out_shape=jax.ShapeDtypeStruct((C, rows, cols), f32),
        in_specs=[spec] * 7 + [pl.BlockSpec(memory_space=pltpu.SMEM)],
        out_specs=pl.BlockSpec(memory_space=pl.ANY),
        scratch_shapes=[
            vm((C, J - 1, rows, cols), bf),
            vm((N, R, rows, LANES), bf),
            vm((N, R - 1, rows, LANES), bf),
            vm((N, H, LANES), f32),
            vm((N, H, LANES), bf),
            vm((N, H, LANES), bf),
            vm((N, H, LANES), bf),
            vm((N, H, LANES), bf),
            vm((N, R - 1, rows, LANES), bf),
            vm((C, rows, J * R * M * LANES), bf),
            vm((C, rows, cols), f32),
            dma((C, J - 1)), dma((C, J - 1)),
            dma((N, R - 1)), dma((N, R - 1)),
            dma((N,)), dma((N,)), dma((N,)), dma((N,)),
            dma((N, R - 1)), dma((N, R - 1)),
            dma((N, R, J - 1)), dma((N, R, J - 1)),
            dma((C,)),
        ],
        compiler_params=pltpu.CompilerParams(
            collective_id=0, has_side_effects=True, vmem_limit_bytes=60 * 1024 * 1024),
    )(blended, twf, twb, thf, tht, dd, ee, cpl)
    return result[None]


def solution(mesh):
    placed = (P(("win", "tm"), None, "row", "col"), P(("win", "tm"), "row", "col"), P("win"))
    return jax.shard_map(
        local,
        mesh=mesh,
        in_specs=placed,
        out_specs=P(("win", "tm"), None, "row", "col"),
        check_vma=False,
    )
```

```python
import functools
import math

import jax
import jax.numpy as jnp
from jax import lax
from jax.experimental import pallas as pl
from jax.experimental.pallas import tpu as pltpu
from jax.sharding import PartitionSpec as P

screen = 0.001
LANES = 128
STEP = 32
HOP = 2
MESH = pl.DeviceIdType.MESH


def scales_of(length_all, mode_ids, valid=None):
    scales = jnp.where(
        mode_ids == 0, math.sqrt(1.0 / length_all), math.sqrt(2.0 / length_all)
    ).astype(jnp.float32)
    return scales if valid is None else jnp.where(valid, scales, 0.0)


def angles_of(length_all, products):
    return (products % (4 * length_all)).astype(jnp.float32) * (math.pi / (2.0 * length_all))


def turn(length_all, products):
    angles = angles_of(length_all, products)
    return jnp.cos(angles), jnp.sin(angles)


def row_table(length_all, mode_ids, scales):
    step = 24
    coarse = 2 * step * jnp.arange(length_all // step, dtype=jnp.int32)[:, None]
    fine = 2 * jnp.arange(step, dtype=jnp.int32)[:, None] + 1
    cos_a, sin_a = turn(length_all, coarse * mode_ids)
    cos_b, sin_b = turn(length_all, fine * mode_ids)
    table = cos_a[:, None] * (cos_b * scales) - sin_a[:, None] * (sin_b * scales)
    return table.reshape(length_all, -1).astype(jnp.bfloat16)


def laplace_eigen(length_all, mode_ids):
    sines = jnp.sin(mode_ids.astype(jnp.float32) * (math.pi / (2.0 * length_all)))
    return 4.0 * sines * sines


def kernel(J, R, n, C, M, seams, grid, fca, fsa, fcb, fsb, bca, bsa, bcb, bsb, thf, tht,
           er, ec, own, other, o_ref, x_ref, twf, twb, dd, ee, xg, sw, sr, u, yb, yin, zin, xb, rb, rg, out,
           g_s, g_r, f_s, f_r, y_s, y_r, z_r, x_s, b_s, b_r, c_s, c_r, o_s):
    j, r, t = lax.axis_index("col"), lax.axis_index("row"), lax.axis_index("tm")
    N = C * M
    left = t < n // 2
    p = jnp.where(left, t, n - 1 - t)
    inner = jnp.where(left, t + 1, t - 1)
    outer = jnp.where(left, t - 1, t + 1)
    edge = p == 0
    mid = p == n // 2 - 1

    half = n // 2
    cols = seams.shape[2]
    blocks_each = J * R * LANES // STEP

    def blend(c):
        x_ref[c] = (seams[c].astype(jnp.float32) * grid[...]).astype(jnp.bfloat16)

    def build_forward(m):
        fine = [(fcb[d, m], fsb[d, m]) for d in range(J)]

        def part(a, carry):
            at = pl.ds(pl.multiple_of(a * STEP, STEP), STEP)
            cos_a, sin_a = fca[m, pl.ds(a, 1), :], fsa[m, pl.ds(a, 1), :]
            for d in range(J):
                twf[d, m, at, :] = (cos_a * fine[d][0] - sin_a * fine[d][1]).astype(jnp.bfloat16)
            return carry

        lax.fori_loop(0, cols // STEP, part, 0)

    def block_of(g):
        return bca[pl.ds(g, 1), :] * bcb[...] - bsa[pl.ds(g, 1), :] * bsb[...]

    def build_backward(m):
        def part(k, carry):
            g = m * blocks_each + k
            at = pl.ds(pl.multiple_of(g * STEP, STEP), STEP)
            twb[at, :] = block_of(g).astype(jnp.bfloat16)
            return carry

        lax.fori_loop(0, blocks_each, part, 0)

        @pl.when(m == 0)
        def _():
            first = lax.broadcasted_iota(jnp.int32, (STEP, cols), 0) == 0
            fixed = block_of(0) * jnp.where(first, math.sqrt(0.5), 1.0)
            twb[0:STEP, :] = fixed.astype(jnp.bfloat16)

    def build_pivots(m):
        a = er[...] + ec[m]

        def sweep(chain):
            rest, first = None, None
            for k in range(half):
                base = a if k == 0 else a + chain[k] * rest
                inverse = 1.0 / (base + chain[k + 1])
                first = inverse if k == 0 else jnp.where(p == k, inverse, first)
                rest = base * inverse
            return base, rest, first

        base, _, first = sweep(own)
        _, rest_other, _ = sweep(other)
        dd[m] = first
        ee[m] = jnp.where(p == half - 1, 1.0 / (base + own[half] * rest_other), first)

    below, above = own[p], own[p + 1]
    blend(0)
    barrier = pltpu.get_barrier_semaphore()
    for d in range(1, J):
        pl.semaphore_signal(barrier, 1, device_id={"col": lax.rem(j + d, J)}, device_id_type=MESH)
    for d in range(1, R):
        pl.semaphore_signal(barrier, 1, device_id={"row": lax.rem(r + d, R)}, device_id_type=MESH)
    pl.semaphore_signal(barrier, 1, device_id={"tm": inner}, device_id_type=MESH)

    @pl.when(p > 0)
    def _():
        pl.semaphore_signal(barrier, 1, device_id={"tm": outer}, device_id_type=MESH)
        pl.semaphore_wait(barrier, J + R)

    @pl.when(p == 0)
    def _():
        pl.semaphore_wait(barrier, J + R - 1)

    def remote(src, dst, ss, rs, where):
        return pltpu.make_async_remote_copy(
            src_ref=src, dst_ref=dst, send_sem=ss, recv_sem=rs,
            device_id=where, device_id_type=MESH)

    def slot(jj, rr, m):
        return pl.ds(pl.multiple_of(((jj * R + rr) * M + m) * LANES, LANES), LANES)

    def gather(c, d):
        return remote(x_ref.at[c], xg.at[c, d - 1], g_s.at[c, d - 1], g_r.at[c, d - 1],
                      {"col": lax.rem(j + d, J)})

    def row_out(i, d):
        peer = lax.rem(r + d, R)
        return remote(sw.at[i, peer], sr.at[i, d - 1], f_s.at[i, d - 1], f_r.at[i, d - 1],
                      {"row": peer})

    def y_inner(i):
        return remote(yb.at[i], yin.at[i], y_s.at[i], y_r.at[i], {"tm": inner})

    def y_middle(i):
        return remote(yb.at[i], zin.at[i], y_s.at[i], z_r.at[i], {"tm": inner})

    def x_outer(i):
        return remote(xb.at[i], zin.at[i], x_s.at[i], z_r.at[i], {"tm": outer})

    def row_back(i, c, m, d):
        return remote(rb.at[i, d - 1], rg.at[c, :, slot(j, r, m)], b_s.at[i, d - 1],
                      b_r.at[i, d - 1], {"row": lax.rem(r + d, R)})

    def col_share(i, c, m, d, e):
        part = rg.at[c, :, slot(j, lax.rem(r + R - d, R), m)]
        return remote(part, part, c_s.at[i, d, e - 1], c_r.at[i, d, e - 1],
                      {"col": lax.rem(j + e, J)})

    def out_copy(c):
        return pltpu.make_async_copy(out.at[c], o_ref.at[c], o_s.at[c])

    for c in range(C):
        if c:
            blend(c)
        for d in range(1, J):
            gather(c, d).start()
        if c == 0:
            build_forward(0)

    def dot(a, b):
        return jnp.dot(a, b, preferred_element_type=jnp.float32)

    def step(i, carry):
        @pl.when(i < N)
        def _():
            c, m = i // M, i % M

            @pl.when((i > 0) & (i < M))
            def _():
                build_forward(i)

            @pl.when(m == 0)
            def _():
                for d in range(1, J):
                    gather(c, d).wait_recv()
            acc = dot(x_ref[c], twf[0, m])
            for d in range(1, J):
                acc += dot(xg[c, d - 1], twf[d, m])
            low = acc.astype(jnp.bfloat16)
            for rr in range(R):
                sw[i, rr] = low[:, rr * LANES:(rr + 1) * LANES]
            for d in range(1, R):
                row_out(i, d).start()

            @pl.when(i < M)
            def _():
                build_pivots(i)

            @pl.when((i >= M) & (i < 2 * M))
            def _():
                build_backward(i - M)

        ib = i - 1

        @pl.when((ib >= 0) & (ib < N))
        def _():
            acc = dot(thf[r], sw[ib, r])
            for d in range(1, R):
                row_out(ib, d).wait_recv()
                acc += dot(thf[lax.rem(r + R - d, R)], sr[ib, d - 1])
            u[ib] = acc

        ic = i - 1 - HOP * p

        @pl.when((ic >= 0) & (ic < N))
        def _():
            @pl.when(p > 0)
            def _():
                y_inner(ic).wait_recv()
                u[ic] = u[ic] + below * yin[ic].astype(jnp.float32)
            yb[ic] = (u[ic] * dd[ic % M]).astype(jnp.bfloat16)

            @pl.when(mid)
            def _():
                y_middle(ic).start()

            @pl.when(jnp.logical_not(mid))
            def _():
                y_inner(ic).start()

        ix = i - 1 - HOP * (n - 1 - p)

        @pl.when((ix >= 0) & (ix < N))
        def _():
            c, m = ix // M, ix % M
            x_outer(ix).wait_recv()
            x = ((u[ix] + above * zin[ix].astype(jnp.float32)) * ee[m]).astype(jnp.bfloat16)
            xb[ix] = x

            @pl.when(p > 0)
            def _():
                x_outer(ix).start()
            for d in range(1, R):
                rb[ix, d - 1] = dot(tht[lax.rem(r + d, R)], x).astype(jnp.bfloat16)
                row_back(ix, c, m, d).start()
            rg[c, :, slot(j, r, m)] = dot(tht[r], x).astype(jnp.bfloat16)
            for e in range(1, J):
                col_share(ix, c, m, 0, e).start()

        iw = ix - 1

        @pl.when((iw >= 0) & (iw < N))
        def _():
            c, m = iw // M, iw % M
            for d in range(1, R):
                row_back(iw, c, m, d).wait_recv()
                for e in range(1, J):
                    col_share(iw, c, m, d, e).start()

        ig = ix - 2

        @pl.when((ig >= 0) & (ig < N))
        def _():
            c, m = ig // M, ig % M
            for d in range(R):
                for e in range(1, J):
                    col_share(ig, c, m, d, e).wait_recv()

            @pl.when(m == M - 1)
            def _():
                out[c] = dot(rg[c], twb[...])
                out_copy(c).start()
        return carry

    lax.fori_loop(0, N + HOP * (n - 1) + 3, step, 0)

    def drain(i, carry):
        c, m = i // M, i % M
        for d in range(1, R):
            row_out(i, d).wait_send()
            row_back(i, c, m, d).wait_send()
        for d in range(R):
            for e in range(1, J):
                col_share(i, c, m, d, e).wait_send()
        y_inner(i).wait_send()

        @pl.when(p > 0)
        def _():
            x_outer(i).wait_send()
        return carry

    lax.fori_loop(0, N, drain, 0)
    for c in range(C):
        for d in range(1, J):
            gather(c, d).wait_send()
        out_copy(c).wait()


def local(seams, levels, weights):
    _, C, rows, cols = seams.shape
    R, J, n = lax.axis_size("row"), lax.axis_size("col"), lax.axis_size("tm")
    j, r, t = lax.axis_index("col"), lax.axis_index("row"), lax.axis_index("tm")
    H, W = rows * R, cols * J
    tile_rows, tile_cols = rows // levels.shape[1], cols // levels.shape[2]
    grid = levels[0].astype(jnp.float32) * 0.25
    grid = jnp.broadcast_to(
        grid[:, None, :, None], (levels.shape[1], tile_rows, levels.shape[2], tile_cols)
    ).reshape(rows, cols)
    modes = W // (J * R)
    M = -(-modes // LANES)
    N = C * M
    lanes = jnp.arange(M * LANES, dtype=jnp.int32).reshape(M, LANES)
    valid = lanes < modes
    blocks = jnp.arange(R, dtype=jnp.int32)[None, :, None] * modes
    mode_f = (j * R * modes + blocks + lanes[:, None, :]).reshape(M, R * LANES)
    valid_f = jnp.broadcast_to(valid[:, None, :], (M, R, LANES)).reshape(M, R * LANES)
    scale_f = scales_of(W, mode_f, valid_f)
    coarse = 2 * STEP * jnp.arange(cols // STEP, dtype=jnp.int32)[:, None]
    fca, fsa = turn(W, coarse * mode_f[:, None])
    firsts = jnp.stack([lax.rem(j + J - d, J) * cols for d in range(J)])
    fine = 2 * (firsts[:, None] + jnp.arange(STEP, dtype=jnp.int32)) + 1
    fcb, fsb = (v * scale_f[None, :, None] for v in turn(W, fine[:, None, :, None] * mode_f[None, :, None]))

    bases = (jnp.arange(J * R, dtype=jnp.int32)[:, None] * modes
             + jnp.arange(M * LANES // STEP, dtype=jnp.int32)[None, :] * STEP).reshape(-1)
    odd = 2 * (j * cols + jnp.arange(cols, dtype=jnp.int32))[None, :] + 1
    bca, bsa = turn(W, bases[:, None] * odd)
    bcb, bsb = (v * math.sqrt(2.0 / W) for v in turn(W, jnp.arange(STEP, dtype=jnp.int32)[:, None] * odd))

    mode_h = jnp.arange(H, dtype=jnp.int32)
    tht = row_table(H, mode_h, scales_of(H, mode_h))
    thf = tht.T.reshape(H, R, rows).transpose(1, 0, 2)
    tht = tht.reshape(R, rows, H)

    own_modes = (j * R + r) * modes + lanes
    er = jnp.broadcast_to((screen + laplace_eigen(H, mode_h))[:, None], (H, LANES))
    ec = laplace_eigen(W, own_modes)[:, None, :]
    stiff = weights.astype(jnp.float32) / 256.0
    couple = 2.0 * stiff[:-1] * stiff[1:] / (stiff[:-1] + stiff[1:])
    left = t < n // 2
    ends = jnp.concatenate([jnp.zeros((1,), jnp.float32), couple])
    flipped = jnp.concatenate([jnp.zeros((1,), jnp.float32), couple[::-1]])
    own = jnp.where(left, ends, flipped)
    other = jnp.where(left, flipped, ends)

    bf, f32 = jnp.bfloat16, jnp.float32
    vm, dma = pltpu.VMEM, pltpu.SemaphoreType.DMA
    spec = pl.BlockSpec(memory_space=pltpu.VMEM)
    result = pl.pallas_call(
        functools.partial(kernel, J, R, n, C, M),
        out_shape=jax.ShapeDtypeStruct((C, rows, cols), f32),
        in_specs=[spec] * 14 + [pl.BlockSpec(memory_space=pltpu.SMEM)] * 2,
        out_specs=pl.BlockSpec(memory_space=pl.ANY),
        scratch_shapes=[
            vm((C, rows, cols), bf),
            vm((J, M, cols, R * LANES), bf),
            vm((J * R * M * LANES, cols), bf),
            vm((M, H, LANES), f32),
            vm((M, H, LANES), f32),
            vm((C, J - 1, rows, cols), bf),
            vm((N, R, rows, LANES), bf),
            vm((N, R - 1, rows, LANES), bf),
            vm((N, H, LANES), f32),
            vm((N, H, LANES), bf),
            vm((N, H, LANES), bf),
            vm((N, H, LANES), bf),
            vm((N, H, LANES), bf),
            vm((N, R - 1, rows, LANES), bf),
            vm((C, rows, J * R * M * LANES), bf),
            vm((C, rows, cols), f32),
            dma((C, J - 1)), dma((C, J - 1)),
            dma((N, R - 1)), dma((N, R - 1)),
            dma((N,)), dma((N,)), dma((N,)), dma((N,)),
            dma((N, R - 1)), dma((N, R - 1)),
            dma((N, R, J - 1)), dma((N, R, J - 1)),
            dma((C,)),
        ],
        compiler_params=pltpu.CompilerParams(
            collective_id=0, has_side_effects=True, vmem_limit_bytes=48 * 1024 * 1024),
    )(seams[0], grid, fca, fsa, fcb, fsb, bca, bsa, bcb, bsb, thf, tht, er, ec, own, other)
    return result[None]


def solution(mesh):
    placed = (P(("win", "tm"), None, "row", "col"), P(("win", "tm"), "row", "col"), P("win"))
    return jax.shard_map(
        local,
        mesh=mesh,
        in_specs=placed,
        out_specs=P(("win", "tm"), None, "row", "col"),
        check_vma=False,
    )
```
